256 devices in a mesh: lon: 16 (over x_lo, z), lat: 16 (over y, x_hi, core).
Axes of the slice: x: 4 (x_hi: 2, x_lo: 2; x = x_hi * 2 + x_lo), y: 4, z: 8, core: 2. Of those that a mesh axis runs over, the one named last changes fastest.
Arguments:
- ensemble: bfloat16 [40, 2, 2048, 4096], P(None, None, 'lat', 'lon'), may hold values from -6 to 6
- gradient: bfloat16 [2, 2048, 4096], P(None, 'lat', 'lon'), may hold values from -6 to 6
Outputs:
- control: bfloat16 [40, 2, 2048, 4096], P(None, None, 'lat', 'lon')
The draws below stay inside these ranges and needn't reach their ends.
All inputs are finite; a program needn't handle non-finite values.
Results may differ from the reference program's by a relative error of at most 0.0073.
Values may be sent and summed in bfloat16 or wider, within the bound.
A program may use at most 128 MiB of HBM per device.

```python
import jax
import jax.numpy as jnp
from jax import lax

MEMBERS = 40
LEV = 2
HALF = 30
LON_DEV = 256
LAT_DEV = 128
NLON = 4096
NLAT = 2048


def level_of(stream_key, extent, cuts, least, high):
    def one(position, parts):
        steps = jax.random.uniform(jax.random.fold_in(jax.random.fold_in(stream_key, 6), position), (parts,), jnp.float32, least / len(cuts), high / len(cuts))
        return jnp.repeat(jnp.exp(steps), extent[position] // parts).reshape((-1,) + (1,) * (len(extent) - position - 1))

    level = one(*cuts[0])
    for cut in cuts[1:]:
        level = level * one(*cut)
    return level


def noise(rng, dims, scale, most, pieces=(), kind=jnp.bfloat16):
    result = jax.random.normal(rng, dims, jnp.float32) * scale
    if len(pieces) > 0:
        result = level_of(rng, dims, pieces, -0.22, 0.18) * result
    return jnp.clip(result, min=-most, max=most).astype(kind)


def setup_inputs(seed: int = 0) -> dict:
    splits = jax.random.split(jax.random.key(seed), 3)
    return {
        "ensemble": noise(splits[0], (MEMBERS, LEV, NLAT, NLON), 1.0, 6.0, ((2, 16), (3, 16))),
        "gradient": noise(splits[1], (LEV, NLAT, NLON), 1.0, 6.0, ((1, 16), (2, 16))),
    }


def kernel_matrix(block_len, half_width):
    spread = 1.0 * half_width
    row_index = jnp.arange(block_len + 2 * half_width)[:, None]
    col_index = jnp.arange(block_len)[None, :]
    offset = (row_index - col_index - half_width).astype(jnp.float32)
    offsets = jnp.arange(-half_width, half_width + 1).astype(jnp.float32)
    normalizer = jnp.sqrt(jnp.sum(jnp.exp(-offsets * offsets / (spread * spread))))
    weights = jnp.where(jnp.abs(offset) <= half_width, jnp.exp(-offset * offset / (2.0 * spread * spread)), 0.0) / normalizer
    return weights.astype(jnp.bfloat16)

def reference(ensemble, gradient):
    lon_kernel = kernel_matrix(LON_DEV, HALF).astype(jnp.float32)
    lat_kernel = kernel_matrix(LAT_DEV, HALF).astype(jnp.float32)
    gradient_f32 = gradient.astype(jnp.float32)
    highest = lax.Precision.HIGHEST

    def member(perturbation):
        product = (perturbation.astype(jnp.float32) * gradient_f32).astype(jnp.bfloat16)
        product = lax.optimization_barrier(product).astype(jnp.float32)
        lon_blocks = NLON // LON_DEV
        filler = jnp.zeros((LEV, NLAT, LON_DEV - 2 * HALF), jnp.float32)
        padded = jnp.concatenate([product[:, :, NLON - HALF:], product, product[:, :, :HALF], filler], axis=2)
        blocks = padded.reshape(LEV, NLAT, lon_blocks + 1, LON_DEV)
        lon_done = jnp.einsum('lanp,pq->lanq', blocks[:, :, :-1], lon_kernel[:LON_DEV], precision=highest)
        lon_done = lon_done + jnp.einsum('lanp,pq->lanq', blocks[:, :, 1:, :2 * HALF], lon_kernel[LON_DEV:], precision=highest)
        lon_done = lon_done.reshape(LEV, NLAT, NLON).astype(jnp.bfloat16)
        lon_done = lax.optimization_barrier(lon_done).astype(jnp.float32)
        lat_blocks = NLAT // LAT_DEV
        padded = jnp.pad(lon_done, ((0, 0), (HALF, LAT_DEV - HALF), (0, 0)))
        blocks = padded.reshape(LEV, lat_blocks + 1, LAT_DEV, NLON)
        across = jnp.einsum('lnpc,pq->lnqc', blocks[:, :-1], lat_kernel[:LAT_DEV], precision=highest)
        across = across + jnp.einsum('lnpc,pq->lnqc', blocks[:, 1:, :2 * HALF], lat_kernel[LAT_DEV:], precision=highest)
        return across.reshape(LEV, NLAT, NLON).astype(jnp.bfloat16)
    return lax.map(member, ensemble)
```

```python
import functools

import jax
import jax.numpy as jnp
import ml_dtypes
import numpy as np
from jax import lax
from jax.experimental import pallas as pl
from jax.experimental.pallas import tpu as pltpu
from jax.sharding import PartitionSpec as P

HALF = 30
GROUP = 8
SLOT = 32
WINDOW = 48
LON_AHEAD = 3
LAT_AHEAD = 3
MESH = pl.DeviceIdType.MESH
F32 = jnp.float32
BF16 = jnp.bfloat16


def kernel_values():
    offsets = np.arange(-HALF, HALF + 1, dtype=np.float64)
    normalizer = np.sqrt(np.sum(np.exp(-offsets * offsets / HALF**2)))
    values = np.exp(-offsets * offsets / (2.0 * HALF**2)) / normalizer
    return values.astype(np.float32).astype(ml_dtypes.bfloat16).astype(np.float32)


def banded(sources, targets):
    values = kernel_values()
    offset = sources - targets
    return np.where(np.abs(offset) <= HALF, values[np.clip(offset + HALF, 0, 2 * HALF)], 0.0)


def window_start(field, rows):
    return min(HALF * field // 16 * 16, rows - WINDOW)


def constants(lat_rows, lon_width):
    columns = np.arange(lon_width)
    lon = np.zeros((4, 2 * lon_width, lon_width), np.float32)
    for j in range(4):
        lon[j, :lon_width] = banded(columns[:, None], columns[None, :])
        first = lon_width + SLOT * j
        halo = np.arange(HALF)
        lon[j, first : first + HALF] = banded(halo[:, None] - HALF, columns[None, :])
        first += lon_width // 2
        lon[j, first : first + HALF] = banded(halo[:, None] + lon_width, columns[None, :])
    rows = np.arange(lat_rows)
    halo = np.arange(HALF)
    packed = GROUP * HALF
    lat = np.zeros((GROUP, lat_rows, lat_rows + 2 * WINDOW), np.float32)
    for j in range(GROUP):
        lat[j, :, :lat_rows] = banded(rows[None, :], rows[:, None])
        first = lat_rows + HALF * j - window_start(j, packed)
        lat[j, :, first : first + HALF] = banded(halo[None, :] - HALF, rows[:, None])
        first += WINDOW
        lat[j, :, first : first + HALF] = banded(halo[None, :] + lat_rows, rows[:, None])
    pick = np.zeros((2, packed, GROUP * 32), np.float32)
    for j in range(GROUP):
        for i in range(HALF):
            pick[0, HALF * j + i, 32 * j + i] = 1.0
            pick[1, HALF * j + i, 32 * j + 32 - HALF + i] = 1.0
    return [a.astype(ml_dtypes.bfloat16) for a in (lon, lat, pick)]


def body(
    n_lon, n_lat, chunks,
    ens_hbm, grad_hbm, lon_hbm, lat_hbm, pick_hbm,
    out_ref,
    ens, grad, lon_k, lat_k, pick, prod, done, lon_send, lon_halo, lat_send, lat_halo,
    const_sem, in_sem, lon_ssem, lon_rsem, lat_ssem, lat_rsem,
):
    lon_at = lax.axis_index("lon")
    lat_at = lax.axis_index("lat")
    lon_low = lax.rem(lon_at + n_lon - 1, n_lon)
    lon_high = lax.rem(lon_at + 1, n_lon)
    has_low = lat_at > 0
    has_high = lat_at < n_lat - 1
    lat_low = jnp.maximum(lat_at - 1, 0)
    lat_high = jnp.minimum(lat_at + 1, n_lat - 1)
    rows, width = prod.shape[1:]
    half = width // 2

    def chunk(c):
        return pl.ds(pl.multiple_of(c * GROUP, GROUP), GROUP)

    def load(c):
        return pltpu.make_async_copy(ens_hbm.at[chunk(c)], ens.at[chunk(c)], in_sem.at[c])

    pairs = ((grad_hbm, grad), (lon_hbm, lon_k), (lat_hbm, lat_k), (pick_hbm, pick))
    fixed = [pltpu.make_async_copy(s, d, const_sem.at[i]) for i, (s, d) in enumerate(pairs)]
    fixed[0].start()
    load(0).start()
    for copy in fixed[1:]:
        copy.start()
    for c in range(1, chunks):
        load(c).start()

    barrier = pltpu.get_barrier_semaphore()
    pl.semaphore_signal(barrier, inc=1, device_id={"lon": lon_low}, device_id_type=MESH)
    pl.semaphore_signal(barrier, inc=1, device_id={"lon": lon_high}, device_id_type=MESH)

    @pl.when(has_low)
    def _():
        pl.semaphore_signal(barrier, inc=1, device_id={"lat": lat_low}, device_id_type=MESH)

    @pl.when(has_high)
    def _():
        pl.semaphore_signal(barrier, inc=1, device_id={"lat": lat_high}, device_id_type=MESH)

    @pl.when(jnp.logical_not(has_low))
    def _():
        lat_halo[0] = jnp.zeros(lat_halo.shape[1:], BF16)

    @pl.when(jnp.logical_not(has_high))
    def _():
        lat_halo[1] = jnp.zeros(lat_halo.shape[1:], BF16)

    def lon_copy(side, c):
        return pltpu.make_async_remote_copy(
            src_ref=lon_send.at[side, c],
            dst_ref=lon_halo.at[side, c],
            send_sem=lon_ssem.at[side, c],
            recv_sem=lon_rsem.at[side, c],
            device_id={"lon": lon_high if side == 0 else lon_low},
            device_id_type=MESH,
        )

    def lat_copy(side, c):
        return pltpu.make_async_remote_copy(
            src_ref=lat_send.at[side, c],
            dst_ref=lat_halo.at[side, c],
            send_sem=lat_ssem.at[side, c],
            recv_sem=lat_rsem.at[side, c],
            device_id={"lat": lat_high if side == 0 else lat_low},
            device_id_type=MESH,
        )

    lane = lax.broadcasted_iota(jnp.int32, (rows, half), 1)

    def product(c):
        load(c).wait()
        for q in range(GROUP // 4):
            low = high = None
            for j in range(4):
                f = c * GROUP + 4 * q + j
                value = (ens[f].astype(F32) * grad[j % 2].astype(F32)).astype(BF16)
                prod[f] = value
                value = value.astype(F32)
                here_low = value[:, :half]
                here_high = pltpu.roll(value[:, half:], (SLOT * j + HALF) % half, 1)
                if j == 0:
                    low, high = here_low, here_high
                else:
                    here_low = pltpu.roll(here_low, SLOT * j, 1)
                    mine = lane >= SLOT * j
                    low = jnp.where(mine, here_low, low)
                    high = jnp.where(mine, here_high, high)
            lon_send[0, c, q] = high.astype(BF16)
            lon_send[1, c, q] = low.astype(BF16)

    def lon_start(c):
        lon_copy(0, c).start()
        lon_copy(1, c).start()

    def lon_sum(c):
        lon_copy(0, c).wait_recv()
        lon_copy(1, c).wait_recv()
        quads = GROUP // 4
        for j in range(4):
            left = [
                jnp.concatenate(
                    [prod[c * GROUP + 4 * q + j], lon_halo[0, c, q], lon_halo[1, c, q]], axis=1
                )
                for q in range(quads)
            ]
            total = jnp.dot(
                jnp.concatenate(left, axis=0), lon_k[j], preferred_element_type=F32
            ).astype(BF16)
            for q in range(quads):
                done[c * GROUP + 4 * q + j] = total[q * rows : (q + 1) * rows]
        first = [done[c * GROUP + j, :32] for j in range(GROUP)]
        last = [done[c * GROUP + j, rows - 32 :] for j in range(GROUP)]
        for side, edge in ((0, last), (1, first)):
            lat_send[side, c] = jnp.dot(
                pick[1 - side], jnp.concatenate(edge, axis=0), preferred_element_type=F32
            ).astype(BF16)

    def lat_start(c):
        @pl.when(has_high)
        def _():
            lat_copy(0, c).start()

        @pl.when(has_low)
        def _():
            lat_copy(1, c).start()

    def lat_sum(c):
        @pl.when(has_low)
        def _():
            lat_copy(0, c).wait_recv()

        @pl.when(has_high)
        def _():
            lat_copy(1, c).wait_recv()

        for j in range(GROUP):
            f = c * GROUP + j
            start = window_start(j, GROUP * HALF)
            right = jnp.concatenate(
                [done[f]] + [lat_halo[side, c, start : start + WINDOW] for side in range(2)],
                axis=0,
            )
            out_ref[f] = jnp.dot(lat_k[j], right, preferred_element_type=F32).astype(BF16)

    fixed[0].wait()
    product(0)
    peers = 2 + has_low.astype(jnp.int32) + has_high.astype(jnp.int32)
    pl.semaphore_wait(barrier, peers)
    lon_start(0)
    for copy in fixed[1:]:
        copy.wait()

    def step(t, carry):
        @pl.when(t < chunks)
        def _():
            product(t)
            lon_start(t)

        at_lon = t - LON_AHEAD

        @pl.when((at_lon >= 0) & (at_lon < chunks))
        def _():
            lon_sum(at_lon)
            lat_start(at_lon)

        at_lat = at_lon - LAT_AHEAD

        @pl.when(at_lat >= 0)
        def _():
            lat_sum(at_lat)

        return carry

    lax.fori_loop(1, chunks + LON_AHEAD + LAT_AHEAD, step, 0)

    def drain(c, carry):
        lon_copy(0, c).wait_send()
        lon_copy(1, c).wait_send()

        @pl.when(has_high)
        def _():
            lat_copy(0, c).wait_send()

        @pl.when(has_low)
        def _():
            lat_copy(1, c).wait_send()

        return carry

    lax.fori_loop(0, chunks, drain, 0)


def shards(n_lon, n_lat, ensemble, gradient):
    members, levels, rows, width = ensemble.shape
    fields = members * levels
    chunks = fields // GROUP
    lon, lat, pick = constants(rows, width)
    packed = GROUP * HALF
    quads = GROUP // 4
    any_space = pl.BlockSpec(memory_space=pl.ANY)
    out = pl.pallas_call(
        functools.partial(body, n_lon, n_lat, chunks),
        out_shape=jax.ShapeDtypeStruct((fields, rows, width), BF16),
        in_specs=[any_space] * 5,
        out_specs=pl.BlockSpec(memory_space=pltpu.VMEM),
        scratch_shapes=[
            pltpu.VMEM((fields, rows, width), BF16),
            pltpu.VMEM(gradient.shape, BF16),
            pltpu.VMEM(lon.shape, BF16),
            pltpu.VMEM(lat.shape, BF16),
            pltpu.VMEM(pick.shape, BF16),
            pltpu.VMEM((fields, rows, width), BF16),
            pltpu.VMEM((fields, rows, width), BF16),
            pltpu.VMEM((2, chunks, quads, rows, width // 2), BF16),
            pltpu.VMEM((2, chunks, quads, rows, width // 2), BF16),
            pltpu.VMEM((2, chunks, packed, width), BF16),
            pltpu.VMEM((2, chunks, packed, width), BF16),
            pltpu.SemaphoreType.DMA((4,)),
            pltpu.SemaphoreType.DMA((chunks,)),
            pltpu.SemaphoreType.DMA((2, chunks)),
            pltpu.SemaphoreType.DMA((2, chunks)),
            pltpu.SemaphoreType.DMA((2, chunks)),
            pltpu.SemaphoreType.DMA((2, chunks)),
        ],
        compiler_params=pltpu.CompilerParams(
            collective_id=0, has_side_effects=True, vmem_limit_bytes=56 * 1024 * 1024
        ),
    )(ensemble.reshape(fields, rows, width), gradient, lon, lat, pick)
    return out.reshape(ensemble.shape)


def solution(mesh):
    placed = (P(None, None, "lat", "lon"), P(None, "lat", "lon"))
    return jax.shard_map(
        functools.partial(shards, mesh.shape["lon"], mesh.shape["lat"]),
        mesh=mesh,
        in_specs=placed,
        out_specs=P(None, None, "lat", "lon"),
        check_vma=False,
    )
```

```python
import functools

import jax
import jax.numpy as jnp
import ml_dtypes
import numpy as np
from jax import lax
from jax.experimental import pallas as pl
from jax.experimental.pallas import tpu as pltpu
from jax.sharding import PartitionSpec as P

HALF = 30
GROUP = 8
SLOT = 32
WINDOW = 48
LON_AHEAD = 6
LAT_AHEAD = 4
DIRECT = 3
ROUTES = 3
RELAY_AFTER = 4
LAG = 3
MESH = pl.DeviceIdType.MESH
F32 = jnp.float32
BF16 = jnp.bfloat16


def kernel_values():
    offsets = np.arange(-HALF, HALF + 1, dtype=np.float64)
    normalizer = np.sqrt(np.sum(np.exp(-offsets * offsets / HALF**2)))
    values = np.exp(-offsets * offsets / (2.0 * HALF**2)) / normalizer
    return values.astype(np.float32).astype(ml_dtypes.bfloat16).astype(np.float32)


def banded(sources, targets):
    values = kernel_values()
    offset = sources - targets
    return np.where(np.abs(offset) <= HALF, values[np.clip(offset + HALF, 0, 2 * HALF)], 0.0)


def window_start(field, rows):
    return min(HALF * field // 16 * 16, rows - WINDOW)


def constants(lat_rows, lon_width):
    columns = np.arange(lon_width)
    lon = np.zeros((4, 2 * lon_width, lon_width), np.float32)
    for j in range(4):
        lon[j, :lon_width] = banded(columns[:, None], columns[None, :])
        first = lon_width + SLOT * j
        halo = np.arange(HALF)
        lon[j, first : first + HALF] = banded(halo[:, None] - HALF, columns[None, :])
        first += lon_width // 2
        lon[j, first : first + HALF] = banded(halo[:, None] + lon_width, columns[None, :])
    rows = np.arange(lat_rows)
    halo = np.arange(HALF)
    packed = GROUP * HALF
    lat = np.zeros((GROUP, lat_rows, lat_rows + 2 * WINDOW), np.float32)
    for j in range(GROUP):
        lat[j, :, :lat_rows] = banded(rows[None, :], rows[:, None])
        first = lat_rows + HALF * j - window_start(j, packed)
        lat[j, :, first : first + HALF] = banded(halo[None, :] - HALF, rows[:, None])
        first += WINDOW
        lat[j, :, first : first + HALF] = banded(halo[None, :] + lat_rows, rows[:, None])
    pick = np.zeros((2, packed, GROUP * 32), np.float32)
    for j in range(GROUP):
        for i in range(HALF):
            pick[0, HALF * j + i, 32 * j + i] = 1.0
            pick[1, HALF * j + i, 32 * j + 32 - HALF + i] = 1.0
    return [a.astype(ml_dtypes.bfloat16) for a in (lon, lat, pick)]


def body(
    n_lon, n_lat, chunks,
    ens_hbm, grad_hbm, lon_hbm, lat_hbm, pick_hbm,
    out_ref,
    ens, grad, lon_k, lat_k, pick, prod, done, lon_send, lon_halo, lat_send, lat_halo,
    relay_box, near_sem, twin_sem, const_sem, in_sem, relay_ssem, relay_rsem, lon_ssem, lon_rsem, lat_ssem, lat_rsem,
):
    lon_at = lax.axis_index("lon")
    lat_at = lax.axis_index("lat")
    lon_low = lax.rem(lon_at + n_lon - 1, n_lon)
    lon_high = lax.rem(lon_at + 1, n_lon)
    has_low = lat_at > 0
    has_high = lat_at < n_lat - 1
    lat_low = jnp.maximum(lat_at - 1, 0)
    lat_high = jnp.minimum(lat_at + 1, n_lat - 1)
    row = n_lon // 2
    place = lax.rem(lon_at, row)
    mine = lon_at - place
    other = row - mine
    upper = place >= row // 2
    relay_side = jnp.where(upper, 0, 1)
    depth = jnp.where(upper, row - 1 - place, place)
    relays = (depth > 0) & (depth <= ROUTES)
    twin = other + place
    toward = mine + jnp.where(upper, jnp.minimum(place + 1, row - 1), jnp.maximum(place - 1, 0))
    relay_to = mine + jnp.where(upper, 0, row - 1)
    rows, width = prod.shape[1:]
    half = width // 2

    def chunk(c):
        return pl.ds(pl.multiple_of(c * GROUP, GROUP), GROUP)

    def load(c):
        return pltpu.make_async_copy(ens_hbm.at[chunk(c)], ens.at[chunk(c)], in_sem.at[c])

    pairs = ((grad_hbm, grad), (lon_hbm, lon_k), (lat_hbm, lat_k), (pick_hbm, pick))
    fixed = [pltpu.make_async_copy(s, d, const_sem.at[i]) for i, (s, d) in enumerate(pairs)]
    fixed[0].start()
    load(0).start()
    for copy in fixed[1:]:
        copy.start()
    for c in range(1, chunks):
        load(c).start()

    barrier = pltpu.get_barrier_semaphore()
    pl.semaphore_signal(barrier, inc=1, device_id={"lon": lon_low}, device_id_type=MESH)
    pl.semaphore_signal(barrier, inc=1, device_id={"lon": lon_high}, device_id_type=MESH)

    @pl.when(depth == 0)
    def _():
        pl.semaphore_signal(barrier, inc=1, device_id={"lon": twin}, device_id_type=MESH)

    @pl.when(has_low)
    def _():
        pl.semaphore_signal(barrier, inc=1, device_id={"lat": lat_low}, device_id_type=MESH)

    @pl.when(has_high)
    def _():
        pl.semaphore_signal(barrier, inc=1, device_id={"lat": lat_high}, device_id_type=MESH)

    @pl.when(jnp.logical_not(has_low))
    def _():
        lat_halo[0] = jnp.zeros(lat_halo.shape[1:], BF16)

    @pl.when(jnp.logical_not(has_high))
    def _():
        lat_halo[1] = jnp.zeros(lat_halo.shape[1:], BF16)

    def lon_copy(side, c):
        return pltpu.make_async_remote_copy(
            src_ref=lon_send.at[side, c],
            dst_ref=lon_halo.at[side, c],
            send_sem=lon_ssem.at[side, c],
            recv_sem=lon_rsem.at[side, c],
            device_id={"lon": lon_high if side == 0 else lon_low},
            device_id_type=MESH,
        )

    def slot(c):
        return jnp.maximum(c - DIRECT, 0) // ROUTES

    def seam_copy(side, c):
        route = 1 + lax.rem(jnp.maximum(c - DIRECT, 0), ROUTES)
        return pltpu.make_async_remote_copy(
            src_ref=lon_send.at[side, c],
            dst_ref=relay_box.at[slot(c)],
            send_sem=lon_ssem.at[side, c],
            recv_sem=relay_rsem.at[slot(c)],
            device_id={"lon": other + (row - 1 - route if side == 0 else route)},
            device_id_type=MESH,
        )

    def relay_copy(c):
        return pltpu.make_async_remote_copy(
            src_ref=relay_box.at[slot(c)],
            dst_ref=lon_halo.at[relay_side, c],
            send_sem=relay_ssem.at[slot(c)],
            recv_sem=lon_rsem.at[relay_side, c],
            device_id={"lon": relay_to},
            device_id_type=MESH,
        )

    def lat_copy(side, c):
        return pltpu.make_async_remote_copy(
            src_ref=lat_send.at[side, c],
            dst_ref=lat_halo.at[side, c],
            send_sem=lat_ssem.at[side, c],
            recv_sem=lat_rsem.at[side, c],
            device_id={"lat": lat_high if side == 0 else lat_low},
            device_id_type=MESH,
        )

    lane = lax.broadcasted_iota(jnp.int32, (rows, half), 1)

    def product(c):
        load(c).wait()
        for q in range(GROUP // 4):
            low = high = None
            for j in range(4):
                f = c * GROUP + 4 * q + j
                value = (ens[f].astype(F32) * grad[j % 2].astype(F32)).astype(BF16)
                prod[f] = value
                value = value.astype(F32)
                here_low = value[:, :half]
                here_high = pltpu.roll(value[:, half:], (SLOT * j + HALF) % half, 1)
                if j == 0:
                    low, high = here_low, here_high
                else:
                    here_low = pltpu.roll(here_low, SLOT * j, 1)
                    mine = lane >= SLOT * j
                    low = jnp.where(mine, here_low, low)
                    high = jnp.where(mine, here_high, high)
            lon_send[0, c, q] = high.astype(BF16)
            lon_send[1, c, q] = low.astype(BF16)

    def seam_start(c):
        for side, end in ((0, row - 1), (1, 0)):

            @pl.when(place == end)
            def _():
                seam_copy(side, c).start()

    def lon_start(c):
        for side, end in ((0, row - 1), (1, 0)):

            @pl.when((place != end) | (c < DIRECT))
            def _():
                lon_copy(side, c).start()

    def relay(c):
        @pl.when(relays & (c >= DIRECT) & (1 + lax.rem(jnp.maximum(c - DIRECT, 0), ROUTES) == depth))
        def _():
            seam_copy(0, c).wait_recv()
            relay_copy(c).start()

    def lon_sum(c):
        lon_copy(0, c).wait_recv()
        lon_copy(1, c).wait_recv()
        quads = GROUP // 4
        for j in range(4):
            left = [
                jnp.concatenate(
                    [prod[c * GROUP + 4 * q + j], lon_halo[0, c, q], lon_halo[1, c, q]], axis=1
                )
                for q in range(quads)
            ]
            total = jnp.dot(
                jnp.concatenate(left, axis=0), lon_k[j], preferred_element_type=F32
            ).astype(BF16)
            for q in range(quads):
                done[c * GROUP + 4 * q + j] = total[q * rows : (q + 1) * rows]
        first = [done[c * GROUP + j, :32] for j in range(GROUP)]
        last = [done[c * GROUP + j, rows - 32 :] for j in range(GROUP)]
        for side, edge in ((0, last), (1, first)):
            lat_send[side, c] = jnp.dot(
                pick[1 - side], jnp.concatenate(edge, axis=0), preferred_element_type=F32
            ).astype(BF16)

    def lat_start(c):
        @pl.when(has_high)
        def _():
            lat_copy(0, c).start()

        @pl.when(has_low)
        def _():
            lat_copy(1, c).start()

    def lat_sum(c):
        @pl.when(has_low)
        def _():
            lat_copy(0, c).wait_recv()

        @pl.when(has_high)
        def _():
            lat_copy(1, c).wait_recv()

        for j in range(GROUP):
            f = c * GROUP + j
            start = window_start(j, GROUP * HALF)
            right = jnp.concatenate(
                [done[f]] + [lat_halo[side, c, start : start + WINDOW] for side in range(2)],
                axis=0,
            )
            out_ref[f] = jnp.dot(lat_k[j], right, preferred_element_type=F32).astype(BF16)

    fixed[0].wait()
    product(0)
    peers = 2 + has_low.astype(jnp.int32) + has_high.astype(jnp.int32)
    peers += jnp.where(depth == 0, 1, 0)
    pl.semaphore_wait(barrier, peers)
    lon_start(0)
    for copy in fixed[1:]:
        copy.wait()

    @pl.when(depth == ROUTES - 1)
    def _():
        pl.semaphore_signal(near_sem, inc=1, device_id={"lon": toward}, device_id_type=MESH)

    def announce():
        @pl.when(depth < ROUTES - 1)
        def _():
            pl.semaphore_wait(near_sem, 1)

        @pl.when((depth > 0) & (depth < ROUTES - 1))
        def _():
            pl.semaphore_signal(near_sem, inc=1, device_id={"lon": toward}, device_id_type=MESH)

        @pl.when(depth == 0)
        def _():
            pl.semaphore_signal(twin_sem, inc=1, device_id={"lon": twin}, device_id_type=MESH)

    def step(t, carry):
        @pl.when(t == 2)
        def _():
            announce()

        @pl.when((t == DIRECT) & (depth == 0))
        def _():
            pl.semaphore_wait(twin_sem, 1)

        @pl.when(t < chunks)
        def _():
            product(t)

            @pl.when(t >= DIRECT)
            def _():
                seam_start(t)

            @pl.when(t < DIRECT)
            def _():
                lon_start(t)

        at_send = t - LAG

        @pl.when((at_send >= DIRECT) & (at_send < chunks))
        def _():
            lon_start(at_send)

        at_lon = t - LON_AHEAD

        @pl.when((at_lon >= 0) & (at_lon < chunks))
        def _():
            lon_sum(at_lon)
            lat_start(at_lon)

        at_relay = t - RELAY_AFTER

        @pl.when((at_relay >= DIRECT) & (at_relay < chunks))
        def _():
            relay(at_relay)

        at_lat = at_lon - LAT_AHEAD

        @pl.when(at_lat >= 0)
        def _():
            lat_sum(at_lat)

        return carry

    lax.fori_loop(1, chunks + LON_AHEAD + LAT_AHEAD, step, 0)

    def drain(c, carry):
        @pl.when(relays & (c >= DIRECT) & (1 + lax.rem(jnp.maximum(c - DIRECT, 0), ROUTES) == depth))
        def _():
            relay_copy(c).wait_send()

        lon_copy(0, c).wait_send()
        lon_copy(1, c).wait_send()

        @pl.when(has_high)
        def _():
            lat_copy(0, c).wait_send()

        @pl.when(has_low)
        def _():
            lat_copy(1, c).wait_send()

        return carry

    lax.fori_loop(0, chunks, drain, 0)


def store(chunks, from_ref, to_ref, sem):
    copies = []
    for c in range(chunks):
        part = pl.ds(c * GROUP, GROUP)
        copies.append(pltpu.make_async_copy(from_ref.at[part], to_ref.at[part], sem.at[c]))
    for copy in copies:
        copy.start()
    for copy in copies:
        copy.wait()


def shards(n_lon, n_lat, ensemble, gradient):
    members, levels, rows, width = ensemble.shape
    fields = members * levels
    chunks = fields // GROUP
    lon, lat, pick = constants(rows, width)
    packed = GROUP * HALF
    quads = GROUP // 4
    in_hbm = pl.BlockSpec(memory_space=pltpu.HBM)
    out = pl.pallas_call(
        functools.partial(body, n_lon, n_lat, chunks),
        out_shape=pltpu.VMEM((fields, rows, width), BF16),
        in_specs=[in_hbm] * 5,
        out_specs=pl.BlockSpec(memory_space=pltpu.VMEM),
        scratch_shapes=[
            pltpu.VMEM((fields, rows, width), BF16),
            pltpu.VMEM(gradient.shape, BF16),
            pltpu.VMEM(lon.shape, BF16),
            pltpu.VMEM(lat.shape, BF16),
            pltpu.VMEM(pick.shape, BF16),
            pltpu.VMEM((fields, rows, width), BF16),
            pltpu.VMEM((fields, rows, width), BF16),
            pltpu.VMEM((2, chunks, quads, rows, width // 2), BF16),
            pltpu.VMEM((2, chunks, quads, rows, width // 2), BF16),
            pltpu.VMEM((2, chunks, packed, width), BF16),
            pltpu.VMEM((2, chunks, packed, width), BF16),
            pltpu.VMEM((pl.cdiv(chunks - DIRECT, ROUTES), quads, rows, width // 2), BF16),
            pltpu.SemaphoreType.REGULAR,
            pltpu.SemaphoreType.REGULAR,
            pltpu.SemaphoreType.DMA((4,)),
            pltpu.SemaphoreType.DMA((chunks,)),
            pltpu.SemaphoreType.DMA((pl.cdiv(chunks - DIRECT, ROUTES),)),
            pltpu.SemaphoreType.DMA((pl.cdiv(chunks - DIRECT, ROUTES),)),
            pltpu.SemaphoreType.DMA((2, chunks)),
            pltpu.SemaphoreType.DMA((2, chunks)),
            pltpu.SemaphoreType.DMA((2, chunks)),
            pltpu.SemaphoreType.DMA((2, chunks)),
        ],
        compiler_params=pltpu.CompilerParams(
            collective_id=0, has_side_effects=True, vmem_limit_bytes=61_700_000
        ),
    )(ensemble.reshape(fields, rows, width), gradient, lon, lat, pick)
    out = pl.pallas_call(
        functools.partial(store, chunks),
        out_shape=jax.ShapeDtypeStruct((fields, rows, width), BF16),
        in_specs=[pl.BlockSpec(memory_space=pltpu.VMEM)],
        out_specs=in_hbm,
        scratch_shapes=[pltpu.SemaphoreType.DMA((chunks,))],
        compiler_params=pltpu.CompilerParams(vmem_limit_bytes=12 * 1024 * 1024),
    )(pltpu.with_memory_space_constraint(out, pltpu.VMEM))
    return out.reshape(ensemble.shape)


def solution(mesh):
    placed = (P(None, None, "lat", "lon"), P(None, "lat", "lon"))
    return jax.shard_map(
        functools.partial(shards, mesh.shape["lon"], mesh.shape["lat"]),
        mesh=mesh,
        in_specs=placed,
        out_specs=P(None, None, "lat", "lon"),
        check_vma=False,
    )
```
